32 devices in a mesh: dom: 8 (over z, core), head: 4 (over y, x).
Axes of the slice: x: 2, y: 2, z: 4, core: 2. Of those that a mesh axis runs over, the one named last changes fastest.
Arguments:
- features: bfloat16 [4096, 1024], P(('dom', 'head')), as said below
- w_query: bfloat16 [1024, 1024], P(None, 'head'), as said below
- w_key: bfloat16 [1024, 1024], P(None, 'head'), as said below
- w_value: bfloat16 [1024, 1024], P(None, 'head'), may hold values from -0.1875 to 0.1875
- w_output: bfloat16 [1024, 1024], P('head'), may hold values from -0.1875 to 0.1875
- cotangent: bfloat16 [4096, 1024], P(('dom', 'head')), may hold values from -6 to 6
- cross_source: int32 [8, 4], P('dom'), may hold values from 0 to 31, as said below
- cross_target: int32 [8, 4], P('dom'), may hold values from 0 to 3, as said below
- cross_count: int32 [8], P('dom'), may hold values from 3 to 4, as said below
Outputs:
- layer_out: bfloat16 [4096, 1024], P(('dom', 'head'))
- grad_features: bfloat16 [4096, 1024], P(('dom', 'head'))
- w_query_grad: float32 [1024, 1024], P('dom', 'head')
- w_key_grad: float32 [1024, 1024], P('dom', 'head')
- w_value_grad: float32 [1024, 1024], P('dom', 'head')
- w_output_grad_t: float32 [1024, 1024], P('dom', 'head')
The draws below stay inside these ranges and needn't reach their ends.
Inputs may be any that keep to these rules, and one draw needn't show every extreme that they name: `cross_source`: row p names global blocks of partitions other than p; at most 2 entries of one row lie in any one partition, and some row has exactly 2 in one partition. `cross_target`: the entries of one row are distinct. `cross_count`: some partition has 4 live slots. `features`: entries lie within 10 in magnitude. `w_query`: entries lie within 5 / sqrt(1024) in magnitude. `w_key`: entries lie within 5 / sqrt(1024) in magnitude.
All inputs are finite; a program needn't handle non-finite values.
Results may differ from the reference program's by a relative error of at most 0.018.
Values may be sent and summed in bfloat16 or wider, within the bound.
No kernel may reach another device: no remote copies, remote signals or barrier semaphores. Data moves between devices by JAX's collectives and lax.ppermute only.
A program may use at most 64 MiB of HBM per device.

```python
import math
import jax
import jax.numpy as jnp
from jax import lax

D = 1024
H = 16
HD = 64
BLK = 128
CAP = 2
PARTS_SIZE = 8
P_NODES = 512
NBLK_P = 4
CMAX = 4
NODES = 4096


def cross_tables(key):
    lowest = CMAX - CMAX // 4
    counts = jax.random.randint(jax.random.fold_in(key, 501), (PARTS_SIZE,), lowest, CMAX + 1)
    full_part = jax.random.randint(jax.random.fold_in(key, 502), (), 0, PARTS_SIZE)
    counts = jnp.where(jnp.arange(PARTS_SIZE) == full_part, CMAX, counts)

    def shuffle_owners(subkey):
        return jax.random.permutation(subkey, PARTS_SIZE - 1)
    owner_order = jax.vmap(shuffle_owners)(jax.random.split(jax.random.fold_in(key, 503), PARTS_SIZE))
    slot_groups = jnp.arange(CMAX) // CAP
    owners = (jnp.arange(PARTS_SIZE)[:, None] + 1 + owner_order[:, slot_groups]) % PARTS_SIZE
    within = jax.random.randint(jax.random.fold_in(key, 504), (PARTS_SIZE, CMAX), 0, NBLK_P)
    source = owners * NBLK_P + within

    def shuffle_slots(subkey):
        return jax.random.permutation(subkey, CMAX)
    slot_order = jax.vmap(shuffle_slots)(jax.random.split(jax.random.fold_in(key, 505), PARTS_SIZE))
    source = jnp.take_along_axis(source, slot_order, axis=1)

    def shuffle_targets(subkey):
        return jax.random.permutation(subkey, NBLK_P)
    target = jax.vmap(shuffle_targets)(jax.random.split(jax.random.fold_in(key, 506), PARTS_SIZE))[:, :CMAX]
    return (source.astype(jnp.int32), target.astype(jnp.int32), counts.astype(jnp.int32))


def draw_cross_source(key, part):
    return cross_tables(key)[0]


def draw_cross_target(key, part):
    return cross_tables(key)[1]


def draw_cross_count(key, part):
    return cross_tables(key)[2]


def projection_pair(key):
    base = jnp.clip(jax.random.normal(jax.random.fold_in(key, 601), (D, D), jnp.float32), -4.0, 4.0) / math.sqrt(D)
    other = jnp.clip(jax.random.normal(jax.random.fold_in(key, 602), (D, D), jnp.float32), -4.0, 4.0) / math.sqrt(D)
    return (base, other)


def draw_w_query(key, part):
    return projection_pair(key)[0].astype(jnp.bfloat16)


def draw_w_key(key, part):
    return projection_pair(key)[1].astype(jnp.bfloat16)


def draw_features(key, part):
    drawn = jax.random.normal(jax.random.fold_in(key, 704), (NODES, D), jnp.float32)
    return jnp.clip(drawn, -4.0, 4.0).astype(jnp.bfloat16)


def strengthened(values, rng, source, target, parts, factor):
    owner, partner = [(jnp.arange(values.shape[dim]) // (values.shape[dim] // parts)).reshape([-1 if axis == dim else 1 for axis in range(values.ndim)]) for dim in (source, target)]
    chosen = jax.random.permutation(rng, parts)[partner]
    strong = (owner == chosen) | (owner == (partner + parts // 2) % parts)
    return jnp.where(strong, factor * values, values)


def steps_of(rng, extent, cuts, smallest, largest):
    def one(dim, blocks):
        steps = jax.random.uniform(jax.random.fold_in(jax.random.fold_in(rng, 6), dim), (blocks,), jnp.float32, smallest / len(cuts), largest / len(cuts))
        return jnp.repeat(jnp.exp(steps), extent[dim] // blocks).reshape((-1,) + (1,) * (len(extent) - dim - 1))

    gain = one(*cuts[0])
    for cut in cuts[1:]:
        gain = gain * one(*cut)
    return gain


def scatter_about(key, dims, scale, reach, cuts=(), held_as=jnp.bfloat16):
    values = jax.random.normal(key, dims, jnp.float32) * scale
    if len(cuts) > 0:
        values = steps_of(key, dims, cuts, -0.22, 0.18) * values
    return jnp.clip(values, min=-reach, max=reach).astype(held_as)


def noise_with(stream_key, dims, scale, limit, shards, heavy, kind=jnp.bfloat16):
    entries = scale * jax.random.normal(stream_key, dims, jnp.float32)
    if shards:
        entries = entries * steps_of(stream_key, dims, shards, -0.22, 0.18)
    return jnp.clip(strengthened(entries, jax.random.fold_in(stream_key, 3), *heavy), -limit, limit).astype(kind)


def setup_inputs(seed: int = 0) -> dict:
    splits = jax.random.split(jax.random.key(seed), 10)
    features = draw_features(jax.random.fold_in(splits[9], 71), 0)
    w_query = draw_w_query(jax.random.fold_in(splits[9], 71), 0)
    w_key = draw_w_key(jax.random.fold_in(splits[9], 71), 0)
    w_value = scatter_about(splits[3], (D, D), D ** -0.5, 0.1875, ((1, 4),))
    w_output = scatter_about(splits[4], (D, D), D ** -0.5, 0.1875, ((0, 4),))
    cotangent = noise_with(splits[5], (NODES, D), 1.0, 6.0, ((0, 32),), (0, 1, 32, 2.75))
    cross_source = draw_cross_source(jax.random.fold_in(splits[9], 71), 0)
    cross_target = draw_cross_target(jax.random.fold_in(splits[9], 71), 0)
    cross_count = draw_cross_count(jax.random.fold_in(splits[9], 71), 0)
    return dict(features=features, w_query=w_query, w_key=w_key, w_value=w_value, w_output=w_output, cotangent=cotangent, cross_source=cross_source, cross_target=cross_target, cross_count=cross_count)


NEG_FILL = -1e+30

def rounded(array):
    return lax.optimization_barrier(array.astype(jnp.bfloat16)).astype(jnp.float32)

def select_table(target, live_count):
    slot_ids = jnp.arange(CMAX, dtype=jnp.int32)
    block_ids = jnp.arange(NBLK_P, dtype=jnp.int32)
    return (target[None, :] == block_ids[:, None]) & (slot_ids < live_count)[None, :]

def gather_extra(chosen, source, key_blocks, value_blocks):
    picker = chosen.astype(jnp.float32)
    extra_keys = jnp.einsum('tj,jbhd->tbhd', picker, key_blocks[source].astype(jnp.float32), precision=lax.Precision.HIGHEST)
    extra_values = jnp.einsum('tj,jbhd->tbhd', picker, value_blocks[source].astype(jnp.float32), precision=lax.Precision.HIGHEST)
    return (extra_keys.astype(jnp.bfloat16), extra_values.astype(jnp.bfloat16))

def part_probs(part_queries, part_keys, extra_keys, usable):
    scaling = 1.0 / math.sqrt(HD)
    query_f = part_queries.astype(jnp.float32)
    local_scores = jnp.einsum('tbhd,nhd->thbn', query_f, part_keys.astype(jnp.float32)) * scaling
    extra_scores = jnp.einsum('tbhd,tehd->thbe', query_f, extra_keys.astype(jnp.float32)) * scaling
    extra_scores = jnp.where(usable[:, None, None, None], extra_scores, NEG_FILL)
    highest = jnp.maximum(lax.optimization_barrier(jnp.max(local_scores, -1)), lax.optimization_barrier(jnp.max(extra_scores, -1)))[..., None]
    local_exp = jnp.exp(local_scores - highest)
    extra_exp = jnp.exp(extra_scores - highest)
    denominator = lax.optimization_barrier(jnp.sum(local_exp, -1, keepdims=True)) + lax.optimization_barrier(jnp.sum(extra_exp, -1, keepdims=True))
    return (local_exp / denominator, extra_exp / denominator)

def reference(features, w_query, w_key, w_value, w_output, cotangent, cross_source, cross_target, cross_count):
    scaling = 1.0 / math.sqrt(HD)
    queries = jnp.dot(features, w_query, preferred_element_type=jnp.float32).astype(jnp.bfloat16)
    keys = jnp.dot(features, w_key, preferred_element_type=jnp.float32).astype(jnp.bfloat16)
    values = jnp.dot(features, w_value, preferred_element_type=jnp.float32).astype(jnp.bfloat16)
    shape_five = (PARTS_SIZE, NBLK_P, BLK, H, HD)
    queries_five = queries.reshape(shape_five)
    keys_part = keys.reshape(PARTS_SIZE, P_NODES, H, HD)
    values_part = values.reshape(PARTS_SIZE, P_NODES, H, HD)
    key_blocks = keys.reshape(PARTS_SIZE * NBLK_P, BLK, H, HD)
    value_blocks = values.reshape(PARTS_SIZE * NBLK_P, BLK, H, HD)

    def part_forward(inputs):
        part_queries, part_keys, part_values, source, target, live_count = inputs
        chosen = select_table(target, live_count)
        extra_keys, extra_values = gather_extra(chosen, source, key_blocks, value_blocks)
        usable = jnp.any(chosen, 1)
        local_probs, extra_probs = part_probs(part_queries, part_keys, extra_keys, usable)
        attended_part = jnp.einsum('thbn,nhd->tbhd', rounded(local_probs), part_values.astype(jnp.float32))
        attended_part = attended_part + jnp.einsum('thbe,tehd->tbhd', rounded(extra_probs), extra_values.astype(jnp.float32))
        return attended_part.astype(jnp.bfloat16)
    attended = lax.map(part_forward, (queries_five, keys_part, values_part, cross_source, cross_target, cross_count))
    attended_flat = attended.reshape(NODES, D)
    layer_out = (features.astype(jnp.float32) + jnp.dot(attended_flat, w_output, preferred_element_type=jnp.float32)).astype(jnp.bfloat16)
    w_output_grad_t = jnp.dot(cotangent.T, attended_flat, preferred_element_type=jnp.float32)
    grad_attended = jnp.dot(cotangent, w_output.T, preferred_element_type=jnp.float32).astype(jnp.bfloat16)
    grad_attended_five = grad_attended.reshape(shape_five)

    def part_backward(inputs):
        part_queries, part_keys, part_values, source, target, live_count, attended_part, grad_part = inputs
        chosen = select_table(target, live_count)
        extra_keys, extra_values = gather_extra(chosen, source, key_blocks, value_blocks)
        usable = jnp.any(chosen, 1)
        local_probs, extra_probs = part_probs(part_queries, part_keys, extra_keys, usable)
        grad_f = grad_part.astype(jnp.float32)
        query_f = part_queries.astype(jnp.float32)
        row_delta = lax.optimization_barrier(jnp.sum(grad_f * attended_part.astype(jnp.float32), -1))
        row_delta = jnp.transpose(row_delta, (0, 2, 1))[..., None]
        local_dprob = jnp.einsum('tbhd,nhd->thbn', grad_f, part_values.astype(jnp.float32))
        extra_dprob = jnp.einsum('tbhd,tehd->thbe', grad_f, extra_values.astype(jnp.float32))
        local_dscore = rounded(local_probs * (local_dprob - row_delta) * scaling)
        extra_dscore = rounded(extra_probs * (extra_dprob - row_delta) * scaling)
        grad_q = jnp.einsum('thbn,nhd->tbhd', local_dscore, part_keys.astype(jnp.float32))
        grad_q = (grad_q + jnp.einsum('thbe,tehd->tbhd', extra_dscore, extra_keys.astype(jnp.float32))).astype(jnp.bfloat16)
        key_local = jnp.einsum('thbn,tbhd->nhd', local_dscore, query_f)
        value_local = jnp.einsum('thbn,tbhd->nhd', rounded(local_probs), grad_f)
        extra_dkey = jnp.einsum('thbe,tbhd->tehd', extra_dscore, query_f)
        extra_dvalue = jnp.einsum('thbe,tbhd->tehd', rounded(extra_probs), grad_f)
        picker = chosen.astype(jnp.float32)
        slot_dkey = jnp.einsum('tj,tehd->jehd', picker, extra_dkey, precision=lax.Precision.HIGHEST)
        slot_dvalue = jnp.einsum('tj,tehd->jehd', picker, extra_dvalue, precision=lax.Precision.HIGHEST)
        return (grad_q, key_local, value_local, slot_dkey, slot_dvalue)
    grad_q, key_local, value_local, slot_dkey, slot_dvalue = lax.map(part_backward, (queries_five, keys_part, values_part, cross_source, cross_target, cross_count, attended, grad_attended_five))
    flat_source = cross_source.reshape(-1)
    key_total = key_local.reshape(PARTS_SIZE * NBLK_P, BLK, H, HD).at[flat_source].add(slot_dkey.reshape(PARTS_SIZE * CMAX, BLK, H, HD))
    value_total = value_local.reshape(PARTS_SIZE * NBLK_P, BLK, H, HD).at[flat_source].add(slot_dvalue.reshape(PARTS_SIZE * CMAX, BLK, H, HD))
    grad_queries = grad_q.reshape(NODES, D)
    grad_keys = key_total.reshape(NODES, D).astype(jnp.bfloat16)
    grad_values = value_total.reshape(NODES, D).astype(jnp.bfloat16)
    back_sum = jnp.dot(grad_queries, w_query.T, preferred_element_type=jnp.float32)
    back_sum = back_sum + jnp.dot(grad_keys, w_key.T, preferred_element_type=jnp.float32)
    back_sum = back_sum + jnp.dot(grad_values, w_value.T, preferred_element_type=jnp.float32)
    grad_features = (cotangent.astype(jnp.float32) + back_sum).astype(jnp.bfloat16)
    w_query_grad = jnp.dot(features.T, grad_queries, preferred_element_type=jnp.float32)
    w_key_grad = jnp.dot(features.T, grad_keys, preferred_element_type=jnp.float32)
    w_value_grad = jnp.dot(features.T, grad_values, preferred_element_type=jnp.float32)
    return (layer_out, grad_features, w_query_grad, w_key_grad, w_value_grad, w_output_grad_t)
```

```python
import functools
import math

import jax
import jax.numpy as jnp
from jax import lax
from jax.experimental import pallas as pl
from jax.experimental.pallas import tpu as pltpu
from jax.sharding import PartitionSpec as P

HD = 64
BLK = 128
NEG_FILL = -1e30
BF16 = jnp.bfloat16
F32 = jnp.float32


def dot(left, right, left_dim=1, right_dim=0):
    return lax.dot_general(
        left, right, (((left_dim,), (right_dim,)), ((), ())), preferred_element_type=F32
    )


def head_swap(pieces):
    n = lax.axis_size("head")
    if n <= 4:
        return [pieces[0]] + [
            lax.ppermute(pieces[k], "head", [(i, i ^ k) for i in range(n)]) for k in range(1, n)
        ]
    order = jnp.arange(n, dtype=jnp.int32) ^ lax.axis_index("head")
    sent = jnp.take(jnp.stack(pieces), order, axis=0)
    received = jnp.take(lax.all_to_all(sent, "head", 0, 0), order, axis=0)
    return [received[k] for k in range(n)]


def head_gather(x):
    return head_swap([x] * lax.axis_size("head"))


def chip_swap(x, k):
    n = lax.axis_size("dom")
    return lax.ppermute(x, "dom", [(i, i ^ (2 * k)) for i in range(n)])


def core_swap(x):
    n = lax.axis_size("dom")
    return lax.ppermute(x, "dom", [(i, i ^ 1) for i in range(n)])


def pick_kernel(which_ref, row_ref, *refs):
    *inputs, out_ref, sems = refs
    total = out_ref.shape[0]

    @pl.loop(0, total)
    def _(t):
        for index, ref in enumerate(inputs):

            @pl.when(which_ref[t] == index)
            def _():
                pltpu.make_async_copy(
                    ref.at[row_ref[t]], out_ref.at[t], sems.at[t]
                ).start()

    @pl.loop(0, total)
    def _(t):
        pltpu.make_async_copy(inputs[0].at[0], out_ref.at[t], sems.at[t]).wait()


def pick(which, row, arrays):
    shape = arrays[0].shape
    return pl.pallas_call(
        pick_kernel,
        name="pick",
        grid_spec=pltpu.PrefetchScalarGridSpec(
            num_scalar_prefetch=2,
            grid=(1,),
            in_specs=[pl.BlockSpec(memory_space=pl.ANY)] * len(arrays),
            out_specs=pl.BlockSpec(shape, lambda i, *_: (0, 0, 0)),
            scratch_shapes=[pltpu.SemaphoreType.DMA((shape[0],))],
        ),
        out_shape=jax.ShapeDtypeStruct(shape, arrays[0].dtype),
    )(which, row, *arrays)


def owned_kernel(place_ref, *refs):
    *inputs, out_ref, acc = refs
    acc[...] = jnp.zeros_like(acc)
    total = inputs[0].shape[0]
    for index, ref in enumerate(inputs):

        @pl.loop(0, total)
        def _(t):
            place = place_ref[index * total + t]

            @pl.when(place >= 0)
            def _():
                acc[place] += ref[t].astype(F32)

    out_ref[...] = acc[...].astype(out_ref.dtype)


def owned(place, arrays, groups):
    total, rows, width = arrays[0].shape
    return pl.pallas_call(
        owned_kernel,
        name="owned",
        grid_spec=pltpu.PrefetchScalarGridSpec(
            num_scalar_prefetch=1,
            grid=(1,),
            in_specs=[pl.BlockSpec((total, rows, width), lambda i, *_: (0, 0, 0))] * len(arrays),
            out_specs=pl.BlockSpec((groups, rows, width), lambda i, *_: (0, 0, 0)),
            scratch_shapes=[pltpu.VMEM((groups, rows, width), F32)],
        ),
        out_shape=jax.ShapeDtypeStruct((groups, rows, width), BF16),
    )(place, *arrays)


def finish_kernel(place_ref, base_ref, *refs):
    *pieces, out_ref, acc = refs
    rows = pieces[0].shape[0]
    acc[...] = base_ref[...]
    for k, piece in enumerate(pieces):
        start = pl.multiple_of(place_ref[k] * rows, rows)
        acc[pl.ds(start, rows), :] += piece[...].astype(F32)
    out_ref[...] = acc[...].astype(out_ref.dtype)


def finish(place, base, pieces):
    whole = pl.BlockSpec(base.shape, lambda i, *_: (0, 0))
    part = pl.BlockSpec(pieces[0].shape, lambda i, *_: (0, 0))
    return pl.pallas_call(
        finish_kernel,
        name="finish",
        grid_spec=pltpu.PrefetchScalarGridSpec(
            num_scalar_prefetch=1,
            grid=(1,),
            in_specs=[whole] + [part] * len(pieces),
            out_specs=whole,
            scratch_shapes=[pltpu.VMEM(base.shape, F32)],
        ),
        out_shape=jax.ShapeDtypeStruct(base.shape, BF16),
    )(place, base, *pieces)


def attention_kernel(
    target_ref,
    usable_ref,
    q_ref,
    k_ref,
    v_ref,
    do_ref,
    kx_ref,
    vx_ref,
    att_ref,
    dq_ref,
    dk_ref,
    dv_ref,
    dkx_ref,
    dvx_ref,
    dk_acc,
    dv_acc,
):
    group = pl.program_id(1)
    width = q_ref.shape[1]
    rows = q_ref.shape[0]
    blocks = rows // BLK
    scaling = 1.0 / math.sqrt(HD)
    lane = lax.broadcasted_iota(jnp.int32, (1, width), 1) // HD
    q = q_ref[...]
    do = do_ref[...]
    k = k_ref[...]
    v = v_ref[...]

    @pl.when(group == 0)
    def _():
        dk_acc[...] = jnp.zeros_like(dk_acc)
        dv_acc[...] = jnp.zeros_like(dv_acc)

    starts = [pl.multiple_of(target_ref[group * blocks + j] * BLK, BLK) for j in range(blocks)]
    usable = [usable_ref[group * blocks + j] > 0 for j in range(blocks)]
    kx = [kx_ref[pl.ds(start, BLK), :] for start in starts]
    vx = [vx_ref[pl.ds(start, BLK), :] for start in starts]
    do_t = jnp.transpose(do.astype(F32))
    att_t = jnp.zeros((width, rows), F32)
    dq_t = jnp.zeros((width, rows), F32)
    dkx = [jnp.zeros((BLK, width), F32) for _ in range(blocks)]
    dvx = [jnp.zeros((BLK, width), F32) for _ in range(blocks)]
    cut = [slice(j * BLK, (j + 1) * BLK) for j in range(blocks)]
    for head in range(width // HD):
        mine = lane == head
        zero = jnp.zeros((), BF16)
        qs = jnp.where(mine, q * jnp.asarray(scaling, BF16), zero)
        do_h = jnp.where(mine, do, zero)
        v_h = jnp.where(mine, v, zero)
        k_h = jnp.where(mine, k, zero)
        score = dot(k, qs, 1, 1)
        extra = jnp.concatenate(
            [
                jnp.where(usable[j], dot(kx[j], qs[cut[j]], 1, 1), NEG_FILL)
                for j in range(blocks)
            ],
            1,
        )
        highest = jnp.maximum(
            jnp.max(score, 0, keepdims=True), jnp.max(extra, 0, keepdims=True)
        )
        probs = jnp.exp(score - highest)
        probs_x = jnp.exp(extra - highest)
        inverse = 1.0 / (jnp.sum(probs, 0, keepdims=True) + jnp.sum(probs_x, 0, keepdims=True))
        probs = probs * inverse
        probs_x = probs_x * inverse
        probs_bf = probs.astype(BF16)
        probs_x_bf = probs_x.astype(BF16)
        out_t = dot(v_h, probs_bf, 0, 0) + jnp.concatenate(
            [
                dot(jnp.where(mine, vx[j], zero), probs_x_bf[:, cut[j]], 0, 0)
                for j in range(blocks)
            ],
            1,
        )
        att_t = att_t + out_t
        delta = jnp.sum(do_t * out_t.astype(BF16).astype(F32), 0, keepdims=True)
        ds = (probs * (dot(v, do_h, 1, 1) - delta)).astype(BF16)
        dprob_x = jnp.concatenate(
            [dot(vx[j], do_h[cut[j]], 1, 1) for j in range(blocks)], 1
        )
        ds_x = (probs_x * (dprob_x - delta)).astype(BF16)
        dq_t = dq_t + dot(k_h, ds, 0, 0) + jnp.concatenate(
            [
                dot(jnp.where(mine, kx[j], zero), ds_x[:, cut[j]], 0, 0)
                for j in range(blocks)
            ],
            1,
        )
        dk_acc[...] += dot(ds, qs)
        dv_acc[...] += dot(probs_bf, do_h)
        for j in range(blocks):
            dkx[j] = dkx[j] + dot(ds_x[:, cut[j]], qs[cut[j]])
            dvx[j] = dvx[j] + dot(probs_x_bf[:, cut[j]], do_h[cut[j]])
    att_ref[...] = jnp.transpose(att_t).astype(BF16)
    dq_ref[...] = (jnp.transpose(dq_t) * scaling).astype(BF16)
    for j in range(blocks):
        dkx_ref[pl.ds(starts[j], BLK), :] = dkx[j].astype(BF16)
        dvx_ref[pl.ds(starts[j], BLK), :] = dvx[j].astype(BF16)

    @pl.when(group == pl.num_programs(1) - 1)
    def _():
        dk_ref[...] = dk_acc[...].astype(BF16)
        dv_ref[...] = dv_acc[...].astype(BF16)


def attention(target, usable, q, k, v, do, kx, vx):
    nodes, columns = q.shape
    width = math.gcd(columns, 2 * HD)
    rows = math.gcd(nodes, max(BLK, 4 * BLK * 4 * BLK // nodes))
    tile = pl.BlockSpec((rows, width), lambda j, g, *_: (g, j))
    full = pl.BlockSpec((nodes, width), lambda j, g, *_: (0, j))
    shape = jax.ShapeDtypeStruct((nodes, columns), BF16)
    return pl.pallas_call(
        attention_kernel,
        name="attention",
        grid_spec=pltpu.PrefetchScalarGridSpec(
            num_scalar_prefetch=2,
            grid=(columns // width, nodes // rows),
            in_specs=[tile, full, full, tile, full, full],
            out_specs=[tile, tile, full, full, full, full],
            scratch_shapes=[pltpu.VMEM((nodes, width), F32)] * 2,
        ),
        out_shape=[shape] * 6,
    )(target, usable, q, k, v, do, kx, vx)


def local(
    features, w_query, w_key, w_value, w_output, cotangent, cross_source, cross_target, cross_count
):
    heads = lax.axis_size("head")
    chips = lax.axis_size("dom") // 2
    part = lax.axis_index("dom")
    mine = lax.axis_index("head")
    chip, core = part // 2, part % 2
    own_rows, model = features.shape
    blocks = heads
    thin = own_rows // heads
    far = range(1, chips)

    source, target, live = cross_source[0], cross_target[0], cross_count[0]
    slots = jnp.arange(source.shape[0], dtype=jnp.int32)
    order = jnp.arange(blocks, dtype=jnp.int32)
    chosen = (target[None, :] == order[:, None]) & (slots < live)[None, :]
    usable = jnp.any(chosen, 1)
    wanted = jnp.sum(jnp.where(chosen, source[None, :], 0), 1)
    table = jnp.where(usable, wanted, -1).astype(jnp.int32).reshape(1, blocks)

    quarters = features.reshape(heads, thin, model)

    def quarter(k):
        return lax.dynamic_index_in_dim(quarters, mine ^ k, 0, keepdims=False)

    strip = jnp.stack(head_swap([quarter(k) for k in range(heads)]))
    strips = [strip] + [chip_swap(strip, k) for k in far]
    strips = strips + [core_swap(s) for s in strips]
    tables = [table] + [chip_swap(table, k) for k in far]
    tables = tables + [core_swap(s) for s in tables]

    owner = wanted // blocks
    which = jnp.where(usable, ((owner % 2) ^ core) * chips + ((owner // 2) ^ chip), chips)
    extra_strip = pick(
        which.astype(jnp.int32), ((wanted % blocks) ^ mine).astype(jnp.int32), strips
    )

    rows = jnp.concatenate(head_gather(features), 0)
    cot = jnp.concatenate(head_gather(cotangent), 0)
    queries = dot(rows, w_query).astype(BF16)
    keys = dot(rows, w_key).astype(BF16)
    values = dot(rows, w_value).astype(BF16)
    grad_attended = dot(cot, w_output, 1, 1).astype(BF16)

    extra_rows = jnp.stack(head_gather(extra_strip), 1)
    extra_rows = extra_rows.reshape(blocks * own_rows, model)
    extra_keys = dot(extra_rows, w_key).astype(BF16)
    extra_values = dot(extra_rows, w_value).astype(BF16)

    attended, grad_q, grad_k, grad_v, grad_kx, grad_vx = attention(
        order ^ mine,
        usable[order ^ mine].astype(jnp.int32),
        queries,
        keys,
        values,
        grad_attended,
        extra_keys,
        extra_values,
    )

    extra_back = (dot(grad_kx, w_key, 1, 1) + dot(grad_vx, w_value, 1, 1)).astype(BF16)
    extra_back = extra_back.reshape(blocks, heads, thin, model)
    slot_back = head_swap([extra_back[:, k] for k in range(heads)])
    slot_back = sum(piece.astype(F32) for piece in slot_back).astype(BF16)
    returned = [slot_back] + [chip_swap(slot_back, k) for k in far]
    returned = returned + [core_swap(s) for s in returned]
    asked = jnp.concatenate(tables[1:], 0)
    place = jnp.where(asked // blocks == part, (asked % blocks) ^ mine, -1)
    place = jnp.where(asked >= 0, place, -1).astype(jnp.int32)
    gathered = owned(place.reshape(-1), returned[1:], heads)
    pieces = head_swap([gathered[k] for k in range(heads)])

    merged = dot(attended, w_output).astype(BF16).reshape(heads, own_rows, model)
    merged = head_swap([merged[k] for k in range(heads)])
    layer_out = sum([piece.astype(F32) for piece in merged], features.astype(F32)).astype(BF16)

    back = (
        dot(grad_q, w_query, 1, 1) + dot(grad_k, w_key, 1, 1) + dot(grad_v, w_value, 1, 1)
    ).astype(BF16).reshape(heads, own_rows, model)
    back = head_swap([back[k] for k in range(heads)])
    base = sum([piece.astype(F32) for piece in back], cotangent.astype(F32))
    ranks = jnp.arange(heads, dtype=jnp.int32)
    grad_features = finish(ranks ^ mine, base, pieces)

    weights = jnp.concatenate(
        [
            dot(rows, grad_q, 0, 0),
            dot(rows, grad_k, 0, 0) + dot(extra_rows, grad_kx, 0, 0),
            dot(rows, grad_v, 0, 0) + dot(extra_rows, grad_vx, 0, 0),
            dot(cot, attended, 0, 0),
        ],
        1,
    ).astype(BF16)
    columns = w_query.shape[1]
    weights = weights.reshape(chips, 2, model // (2 * chips), 4 * columns)
    keep = lax.dynamic_index_in_dim(weights, core, 1, keepdims=False)
    give = lax.dynamic_index_in_dim(weights, 1 - core, 1, keepdims=False)
    paired = keep.astype(F32) + core_swap(give).astype(F32)
    weight_sum = lax.dynamic_index_in_dim(paired, chip, 0, keepdims=False)
    for k in far:
        piece = lax.dynamic_index_in_dim(paired, chip ^ k, 0, keepdims=False)
        weight_sum = weight_sum + chip_swap(piece.astype(BF16), k).astype(F32)
    return (
        layer_out,
        grad_features,
        weight_sum[:, :columns],
        weight_sum[:, columns : 2 * columns],
        weight_sum[:, 2 * columns : 3 * columns],
        weight_sum[:, 3 * columns :],
    )


def solution(mesh):
    return jax.shard_map(
        local,
        mesh=mesh,
        in_specs=(
            P(("dom", "head"), None),
            P(None, "head"),
            P(None, "head"),
            P(None, "head"),
            P("head", None),
            P(("dom", "head"), None),
            P("dom", None),
            P("dom", None),
            P("dom"),
        ),
        out_specs=(
            P(("dom", "head"), None),
            P(("dom", "head"), None),
            P("dom", "head"),
            P("dom", "head"),
            P("dom", "head"),
            P("dom", "head"),
        ),
        check_vma=False,
    )
```
